256 devices in a mesh: row: 32 (over x_lo, z, core), col: 8 (over y, x_hi).
Axes of the slice: x: 4 (x_hi: 2, x_lo: 2; x = x_hi * 2 + x_lo), y: 4, z: 8, core: 2. Of those that a mesh axis runs over, the one named last changes fastest.
Arguments:
- errors: bfloat16 [8192, 8192], P('col', 'row'), may hold values from -0.25 to 0.25
- inputs: bfloat16 [8192, 8192], P('row', 'col'), may hold values from -6 to 6
- weight: float32 [8192, 8192], P('row', 'col'), may hold values from -3 to 3
- weight_moment_one: bfloat16 [8192, 8192], P('row', 'col'), may hold values from -3 to 3
- weight_moment_two: bfloat16 [8192, 8192], P('row', 'col'), may hold values from 0.049804688 to 2
- feedback: float32 [8, 1024, 8192], P(None, 'row', 'col'), may hold values from -3 to 3
- feedback_moment_one: bfloat16 [8, 1024, 8192], P(None, 'row', 'col'), may hold values from -3 to 3
- feedback_moment_two: bfloat16 [8, 1024, 8192], P(None, 'row', 'col'), may hold values from 0.049804688 to 2
Outputs:
- new_weight: float32 [8192, 8192], P('row', 'col')
- new_weight_moment_one: bfloat16 [8192, 8192], P('row', 'col')
- new_weight_moment_two: bfloat16 [8192, 8192], P('row', 'col')
- weight_copy: bfloat16 [8192, 8192], P('row', 'col')
- new_feedback: float32 [8, 1024, 8192], P(None, 'row', 'col')
- new_feedback_moment_one: bfloat16 [8, 1024, 8192], P(None, 'row', 'col')
- new_feedback_moment_two: bfloat16 [8, 1024, 8192], P(None, 'row', 'col')
- feedback_copy: bfloat16 [8, 1024, 8192], P(None, 'row', 'col')
The draws below stay inside these ranges and needn't reach their ends.
All inputs are finite; a program needn't handle non-finite values.
Results may differ from the reference program's by a relative error of at most 0.001.
Values may be sent and summed in bfloat16 or wider, within the bound.
A program may use at most 128 MiB of HBM per device.

```python
import math
import jax
import jax.numpy as jnp
from jax import lax

D = 8192
TOKENS = 8192
N_COL = 8


def block_scale(key, extent, split, smallest, high):
    loudness, own = 1.0, jax.random.fold_in(key, 6)
    for position, shards_of in split:
        steps = jnp.exp(jax.random.uniform(jax.random.fold_in(own, position), (shards_of,), jnp.float32, smallest / len(split), high / len(split)))
        loudness = loudness * jnp.repeat(steps, extent[position] // shards_of).reshape([-1 if axis == position else 1 for axis in range(len(extent))])
    return loudness


def centred(own_key, extent, scale, reach, split=(), held_as=jnp.bfloat16):
    entries = scale * jax.random.normal(own_key, extent, jnp.float32)
    if split:
        entries = entries * block_scale(own_key, extent, split, -0.22, 0.18)
    return jnp.clip(entries, -reach, reach).astype(held_as)


def setup_inputs(seed: int = 0) -> dict:
    splits = jax.random.split(jax.random.key(seed), 9)
    return {
        "errors": centred(splits[0], (TOKENS, D), (TOKENS // 16) ** -0.5, 0.25, ((0, 8), (1, 32))),
        "inputs": centred(splits[1], (TOKENS, D), 1.0, 6.0, ((0, 32), (1, 8))),
        "weight": centred(splits[2], (D, D), 0.5, 3.0, ((0, 32), (1, 8)), jnp.float32),
        "weight_moment_one": centred(splits[3], (D, D), 0.5, 3.0, ((0, 32), (1, 8))),
        "weight_moment_two": jnp.clip(jnp.exp(math.log(2.0) - 3.6927934 * jax.random.uniform(splits[4], (D, D), jnp.float32) ** block_scale(splits[4], (D, D), ((0, 32), (1, 8)), -0.2, 0.2)), 0.049804688, 2.0).astype(jnp.bfloat16),
        "feedback": centred(splits[5], (N_COL, D // N_COL, D), 0.5, 3.0, ((1, 32), (2, 8)), jnp.float32),
        "feedback_moment_one": centred(splits[6], (N_COL, D // N_COL, D), 0.5, 3.0, ((1, 32), (2, 8))),
        "feedback_moment_two": jnp.clip(jnp.exp(math.log(2.0) - 3.6927934 * jax.random.uniform(splits[7], (N_COL, D // N_COL, D), jnp.float32) ** block_scale(splits[7], (N_COL, D // N_COL, D), ((1, 32), (2, 8)), -0.2, 0.2)), 0.049804688, 2.0).astype(jnp.bfloat16),
    }


beta_one = 0.9
beta_two = 0.999
learn_rate = 0.02
decay_rate = 0.1
epsilon = 1e-08
bias_one = 1.0
bias_two = 0.63230458

def adam_update(master, moment_one, moment_two, gradient):
    first_new = beta_one * moment_one.astype(jnp.float32) + (1.0 - beta_one) * gradient
    second_new = beta_two * moment_two.astype(jnp.float32) + (1.0 - beta_two) * gradient * gradient
    update = first_new / bias_one / (jnp.sqrt(second_new / bias_two) + epsilon)
    master_new = master * (1.0 - learn_rate * decay_rate) - learn_rate * update
    return (master_new, first_new.astype(jnp.bfloat16), second_new.astype(jnp.bfloat16), master_new.astype(jnp.bfloat16))

def reference(errors, inputs, weight, weight_moment_one, weight_moment_two, feedback, feedback_moment_one, feedback_moment_two):
    gradient = jnp.dot(errors.astype(jnp.float32).T, inputs.astype(jnp.float32), precision=lax.Precision.HIGHEST)
    w_master, w_first, w_second, w_copy = adam_update(weight, weight_moment_one, weight_moment_two, gradient)
    flipped = gradient.T.reshape(feedback.shape)
    b_master, b_first, b_second, b_copy = adam_update(feedback, feedback_moment_one, feedback_moment_two, flipped)
    return (w_master, w_first, w_second, w_copy, b_master, b_first, b_second, b_copy)
```

```python
import jax
import jax.numpy as jnp
from jax import lax
from jax.experimental import pallas as pl
from jax.experimental.pallas import tpu as pltpu
from jax.sharding import PartitionSpec as P

beta_one = 0.9
beta_two = 0.999
learn_rate = 0.02
decay_rate = 0.1
epsilon = 1e-08
bias_one = 1.0
bias_two = 0.63230458

MESH = pl.DeviceIdType.MESH


def adam_update(master, moment_one, moment_two, gradient):
    first_new = beta_one * moment_one.astype(jnp.float32) + (1.0 - beta_one) * gradient
    second_new = beta_two * moment_two.astype(jnp.float32) + (1.0 - beta_two) * gradient * gradient
    update = first_new / bias_one / (jnp.sqrt(second_new / bias_two) + epsilon)
    master_new = master * (1.0 - learn_rate * decay_rate) - learn_rate * update
    return (
        master_new,
        first_new.astype(jnp.bfloat16),
        second_new.astype(jnp.bfloat16),
        master_new.astype(jnp.bfloat16),
    )


def gradient_kernel(
    err_ref, inp_ref, gw_ref, gb_ref,
    ibuf, ebuf, gt, psend, prec, zrec,
    i_recv, i_send, sib_recv, sib_send, e_recv, x_send, y_send, rs_recv, rs_send, z_recv, z_send, p_recv, p_send,
):
    row, col = lax.axis_index("row"), lax.axis_index("col")
    x_lo, z, core = row // 16, (row // 2) % 8, row % 2
    y, x_hi = col // 2, col % 2
    same = x_lo == y // 2
    odd = y % 2
    near = jnp.where(same, odd, 1 - odd)
    beside = (y + 2 * odd + 3) % 4

    def device(x_lo=x_lo, x_hi=x_hi, y=y, z=z, core=core):
        return (x_lo * 16 + z * 2 + core, y * 2 + x_hi)

    def send(src, dst, send_sem, recv_sem, to):
        return pltpu.make_async_remote_copy(
            src_ref=src, dst_ref=dst, send_sem=send_sem, recv_sem=recv_sem, device_id=to, device_id_type=MESH
        )

    def arrived(ref, sem):
        pltpu.make_async_copy(ref, ref, sem).wait()

    barrier = pltpu.get_barrier_semaphore()

    def greet(to):
        pl.semaphore_signal(barrier, inc=1, device_id=to, device_id_type=MESH)

    @pl.loop(1, 8)
    def _(d):
        greet(device(z=(z + d) % 8))

    greet(device(core=1 - core))
    greet(device(y=y + 1 - 2 * odd))
    greet(device(x_lo=1 - x_lo))

    @pl.when(same)
    def _():
        greet(device(x_lo=1 - x_lo, x_hi=0))
        greet(device(x_lo=1 - x_lo, x_hi=1))
        greet(device(x_hi=1 - x_hi))

    @pl.when(jnp.logical_not(same))
    def _():
        greet(device(y=beside))

    @pl.loop(0, 16)
    def _(n):
        from_y, from_hi, from_core = n // 4, (n // 2) % 2, n % 2
        mine = same & (from_y == y) & (from_hi == x_hi) & (from_core == core)

        @pl.when(jnp.logical_not(mine))
        def _():
            greet(device(x_lo=y // 2, x_hi=from_hi, y=from_y, core=from_core))

    for j in range(4):
        first = (4 * (j // 2) + j % 2) * 128
        ibuf[j, z, core, :, 0:128] = inp_ref[:, first : first + 128]
        ibuf[j, z, core, :, 128:256] = inp_ref[:, first + 256 : first + 384]

    pl.semaphore_wait(barrier, jnp.where(same, 27, 28))

    mine_at = 2 * odd + x_hi

    @pl.when(same)
    def _():
        for s in range(4):
            rows = err_ref.at[pl.ds(256 * s, 256)]
            pltpu.make_async_copy(rows, ebuf.at[x_lo, mine_at, s], e_recv.at[x_lo, mine_at, s]).start()
            send(rows, ebuf.at[x_lo, mine_at, s], x_send.at[0], e_recv.at[x_lo, mine_at, s], device(x_hi=1 - x_hi)).start()

    @pl.when(jnp.logical_not(same))
    def _():
        for s in range(4):
            rows = err_ref.at[pl.ds(256 * s, 256)]
            for h in range(2):
                send(
                    rows, ebuf.at[x_lo, mine_at, s], x_send.at[h], e_recv.at[x_lo, mine_at, s],
                    device(x_lo=1 - x_lo, x_hi=h),
                ).start()

    def up(j, zs):
        s = ibuf.at[j, zs, core]
        send(s, s, i_send.at[0], i_recv.at[j, zs], device(z=(z + 1) % 8)).start()

    def down(j, zs):
        s = ibuf.at[j, zs, core]
        send(s, s, i_send.at[1], i_recv.at[j, zs], device(z=(z + 7) % 8)).start()

    def across(j, zs):
        s = ibuf.at[j, zs, core]
        send(s, s, sib_send.at[j], sib_recv.at[j], device(core=1 - core)).start()

    def inputs_first(g):
        for j in (2 * g, 2 * g + 1):
            up(j, z)
            down(j, z)
        for j in (2 * g, 2 * g + 1):
            across(j, z)

    def inputs_step(g, h):
        for j in (2 * g, 2 * g + 1):
            reach_up, reach_down = 4 - j % 2, 3 + j % 2
            if h <= reach_up:
                zs = (z + 8 - h) % 8
                arrived(ibuf.at[j, zs, core], i_recv.at[j, zs])
                if h < reach_up:
                    up(j, zs)
                across(j, zs)
            if h <= reach_down:
                zs = (z + h) % 8
                arrived(ibuf.at[j, zs, core], i_recv.at[j, zs])
                if h < reach_down:
                    down(j, zs)
                across(j, zs)

    def inputs_ready(j):
        arrived(ibuf.at[j, :, 0], sib_recv.at[j])

    order = [(0, 0), (0, 1)] + [(k, s) for s in range(4) for k in (2, 3)] + [(0, 2), (0, 3)] + [(1, s) for s in range(4)]

    def error_slot(k, s, side):
        own = k < 2
        hi = jnp.where(k == 0, x_hi, 1 - x_hi) if own else k - 2
        return (x_lo if own else 1 - x_lo, 2 * side + hi, s)

    def errors_step(n):
        a, i, s = error_slot(*order[n], near)
        slot = ebuf.at[a, i, s]
        arrived(slot, e_recv.at[a, i, s])
        send(slot, slot, y_send.at[0], e_recv.at[a, i, s], device(y=y + 1 - 2 * odd)).start()

        @pl.when(same)
        def _():
            send(slot, slot, y_send.at[1], e_recv.at[a, i, s], device(y=beside)).start()

    def errors_far(kinds):
        for k, s in order:
            if k in kinds:
                a, i, s = error_slot(k, s, 1 - near)
                arrived(ebuf.at[a, i, s], e_recv.at[a, i, s])

    def product(j, a):
        return lax.dot_general(
            ibuf[j].reshape(4096, 256), ebuf[a].reshape(4096, 256), (((0,), (0,)), ((), ())),
            preferred_element_type=jnp.float32,
        )

    def partial_sums(j):
        psend[j] = product(j, 1 - x_lo)
        send(psend.at[j], prec.at[j], rs_send.at[j], rs_recv.at[j], device(x_lo=1 - x_lo)).start()

    inputs_first(0)
    errors_step(0)
    inputs_step(0, 1)
    errors_step(1)
    errors_step(2)
    inputs_step(0, 2)
    errors_step(3)
    errors_step(4)
    inputs_step(0, 3)
    inputs_first(1)
    errors_step(5)
    errors_step(6)
    inputs_step(0, 4)
    errors_step(7)
    inputs_step(1, 1)
    errors_step(8)
    errors_step(9)
    inputs_step(1, 2)
    inputs_ready(0)
    inputs_ready(1)
    errors_step(10)
    errors_step(11)
    errors_far((2, 3))

    @pl.loop(0, 2)
    def _(j):
        partial_sums(j)

    inputs_step(1, 3)
    errors_step(12)
    errors_step(13)
    inputs_step(1, 4)
    errors_step(14)
    inputs_ready(2)
    inputs_ready(3)

    @pl.loop(2, 4)
    def _(j):
        partial_sums(j)

    errors_step(15)
    errors_far((0, 1))

    @pl.loop(0, 4)
    def _(j):
        total = product(j, x_lo)
        arrived(prec.at[j], rs_recv.at[j])
        gt[j] = (total + prec[j]).reshape(4, 2, 32, 256)
        for q in range(4):
            to_z = 2 * (j % 2) + q % 2 + 4 * (q // 2)
            dst, sem = zrec.at[z, j // 2], z_recv.at[z, j // 2]

            @pl.when(to_z == z)
            def _():
                pltpu.make_async_copy(gt.at[j, q], dst, sem).start()

            @pl.when(to_z != z)
            def _():
                send(gt.at[j, q], dst, z_send.at[j, q], sem, device(z=to_z)).start()

    @pl.loop(0, 4)
    def _(j):
        first = pl.multiple_of((4 * (j // 2) + j % 2) * 128, 128)
        flat = gt[j].reshape(256, 256)
        gw_ref[:, pl.ds(first, 128)] = flat[:128].T
        gw_ref[:, pl.ds(pl.multiple_of(first + 256, 128), 128)] = flat[128:].T

    def onward(n, start):
        step, to_lo = n // 2, n % 2
        zs = (z + jnp.where(step % 2 == 1, (step + 1) // 2, 8 - step // 2)) % 8
        if start:
            arrived(zrec.at[zs, to_lo], z_recv.at[zs, to_lo])
        to_y, to_hi = 2 * x_lo + zs // 4, (zs // 2) % 2
        columns = pl.ds(pl.multiple_of(((zs % 2) * 2 + core) * 256, 256), 256)
        for k in range(2):
            src, dst = zrec.at[zs, to_lo, k], gb_ref.at[col, :, columns]
            mine = (to_lo == x_lo) & (to_hi == x_hi) & (to_y == y) & (core == k)
            if start:
                @pl.when(mine)
                def _():
                    pltpu.make_async_copy(src, dst, p_recv).start()

            @pl.when(jnp.logical_not(mine))
            def _():
                go = send(src, dst, p_send.at[n, k], p_recv, device(x_lo=to_lo, x_hi=to_hi, y=to_y, core=k))
                if start:
                    go.start()
                else:
                    go.wait_send()

    @pl.loop(0, 16)
    def _(n):
        onward(n, True)

    def sent(ref, sem):
        send(ref, ref, sem, sem, device()).wait_send()

    half = ebuf.at[0]
    sent(err_ref, x_send.at[0])
    sent(half, y_send.at[0])

    @pl.when(same)
    def _():
        sent(half, y_send.at[1])

    @pl.when(jnp.logical_not(same))
    def _():
        sent(err_ref, x_send.at[1])

    for d in range(2):
        sent(ibuf.at[0, 0:7], i_send.at[d])
    for j in range(4):
        sent(ibuf.at[j, :, 0], sib_send.at[j])
        sent(psend.at[j], rs_send.at[j])
        for q in range(4):
            to_z = 2 * (j % 2) + q % 2 + 4 * (q // 2)

            @pl.when(to_z != z)
            def _():
                sent(gt.at[j, q], z_send.at[j, q])

    @pl.loop(0, 16)
    def _(n):
        onward(n, False)

    arrived(gb_ref, p_recv)


def gradients(errors, inputs):
    dma = pltpu.SemaphoreType.DMA
    vmem = pl.BlockSpec(memory_space=pltpu.VMEM)
    return pl.pallas_call(
        gradient_kernel,
        out_shape=(
            jax.ShapeDtypeStruct((256, 1024), jnp.float32),
            jax.ShapeDtypeStruct((8, 32, 1024), jnp.float32),
        ),
        in_specs=[vmem, vmem],
        out_specs=(vmem, vmem),
        scratch_shapes=[
            pltpu.VMEM((4, 8, 2, 256, 256), jnp.bfloat16),
            pltpu.VMEM((2, 4, 4, 256, 256), jnp.bfloat16),
            pltpu.VMEM((4, 4, 2, 32, 256), jnp.float32),
            pltpu.VMEM((4, 256, 256), jnp.float32),
            pltpu.VMEM((4, 256, 256), jnp.float32),
            pltpu.VMEM((8, 2, 2, 32, 256), jnp.float32),
            dma((4, 8)), dma((2,)), dma((4,)), dma((4,)),
            dma((2, 4, 4)), dma((2,)), dma((2,)),
            dma((4,)), dma((4,)), dma((8, 2)), dma((4, 4)), dma, dma((16, 2)),
        ],
        compiler_params=pltpu.CompilerParams(
            collective_id=0, has_side_effects=True, vmem_limit_bytes=48 << 20
        ),
        name="gradients",
    )(errors, inputs)


def shards(
    errors,
    inputs,
    weight,
    weight_moment_one,
    weight_moment_two,
    feedback,
    feedback_moment_one,
    feedback_moment_two,
):
    gradient, flipped = gradients(errors, inputs)
    return adam_update(weight, weight_moment_one, weight_moment_two, gradient) + adam_update(
        feedback, feedback_moment_one, feedback_moment_two, flipped
    )


def solution(mesh):
    whole, parts = P("row", "col"), P(None, "row", "col")
    return jax.shard_map(
        shards,
        mesh=mesh,
        in_specs=(P("col", "row"), whole, whole, whole, whole, parts, parts, parts),
        out_specs=(whole,) * 4 + (parts,) * 4,
        check_vma=False,
    )
```

```python
import jax
import jax.numpy as jnp
from jax import lax
from jax.experimental import pallas as pl
from jax.experimental.pallas import tpu as pltpu
from jax.sharding import PartitionSpec as P

beta_one = 0.9
beta_two = 0.999
learn_rate = 0.02
decay_rate = 0.1
epsilon = 1e-08
bias_one = 1.0
bias_two = 0.63230458

MESH = pl.DeviceIdType.MESH


def adam_update(master, moment_one, moment_two, gradient):
    first_new = beta_one * moment_one.astype(jnp.float32) + (1.0 - beta_one) * gradient
    second_new = beta_two * moment_two.astype(jnp.float32) + (1.0 - beta_two) * gradient * gradient
    update = first_new / bias_one / (jnp.sqrt(second_new / bias_two) + epsilon)
    master_new = master * (1.0 - learn_rate * decay_rate) - learn_rate * update
    return (
        master_new,
        first_new.astype(jnp.bfloat16),
        second_new.astype(jnp.bfloat16),
        master_new.astype(jnp.bfloat16),
    )


def gradient_kernel(
    err_ref, inp_ref, gw_ref, gb_ref,
    ibuf, ebuf, rbuf, gt, psend, prec,
    i_recv, i_send, sib_recv, sib_send, e_recv, r_recv, d_send, x_send, y_send, rs_recv, rs_send, p_recv, p_send,
):
    row, col = lax.axis_index("row"), lax.axis_index("col")
    x_lo, z, core = row // 16, (row // 2) % 8, row % 2
    y, x_hi = col // 2, col % 2
    same = x_lo == y // 2
    other = jnp.logical_not(same)
    odd = y % 2
    near = jnp.where(same, odd, 1 - odd)
    pair_y, beside_y = y + 1 - 2 * odd, (y + 2 * odd + 3) % 4
    owner_col = row // 4
    at_home = owner_col == col

    def device(x_lo=x_lo, x_hi=x_hi, y=y, z=z, core=core):
        return (x_lo * 16 + z * 2 + core, y * 2 + x_hi)

    pair, beside, sibling = device(y=pair_y), device(y=beside_y), device(core=1 - core)

    def send(src, dst, send_sem, recv_sem, to):
        pltpu.make_async_remote_copy(
            src_ref=src, dst_ref=dst, send_sem=send_sem, recv_sem=recv_sem, device_id=to, device_id_type=MESH
        ).start()

    def arrived(ref, sem):
        pltpu.make_async_copy(ref, ref, sem).wait()

    def sent(ref, sem):
        pltpu.make_async_remote_copy(
            src_ref=ref, dst_ref=ref, send_sem=sem, recv_sem=sem, device_id=sibling, device_id_type=MESH
        ).wait_send()

    def own_inputs(j):
        unit = lax.broadcasted_iota(jnp.int32, (1024, 256), 0)
        place = lax.broadcasted_iota(jnp.int32, (1024, 256), 1)
        select = jnp.where(unit == (place // 8) * 32 + 8 * j + place % 8, 1.0, 0.0).astype(jnp.bfloat16)
        ibuf[j, z, core] = jnp.dot(inp_ref[...], select, preferred_element_type=jnp.float32).astype(jnp.bfloat16)

    barrier = pltpu.get_barrier_semaphore()

    def greet(to):
        pl.semaphore_signal(barrier, inc=1, device_id=to, device_id_type=MESH)

    greet(device(z=(z + 1) % 8))
    greet(device(z=(z + 7) % 8))
    greet(sibling)
    greet(pair)
    greet(beside)
    for h in range(2):
        greet(device(x_lo=1 - x_lo, x_hi=h))

    @pl.when(same)
    def _():
        greet(device(x_hi=1 - x_hi))

    @pl.loop(0, 32)
    def _(n):
        @pl.when(jnp.logical_not(at_home & (4 * col + n // 8 == row) & (n % 8 == col)))
        def _():
            greet((4 * col + n // 8, n % 8))

    own_inputs(0)
    own_inputs(1)
    pl.semaphore_wait(barrier, 39 + jnp.where(same, 1, 0) - jnp.where(at_home, 1, 0))

    def hop(j, zs, u, way):
        s = ibuf.at[j, zs, core, pl.ds(128 * u, 128)]
        send(s, s, i_send.at[way], i_recv.at[j, zs, u], device(z=(z + (1, 7)[way]) % 8))

    def across(j, zs):
        s = ibuf.at[j, zs, core]
        send(s, s, sib_send.at[j], sib_recv.at[j], sibling)

    def inputs_first(j):
        for u in range(2):
            for way in range(2):
                hop(j, z, u, way)
        across(j, z)

    def inputs_step(group, h):
        for j in group:
            for way in range(2):
                zs = (z + (8 - h, h)[way]) % 8
                for u in range(2):
                    if h < 4 or u == way:
                        arrived(ibuf.at[j, zs, core, pl.ds(128 * u, 128)], i_recv.at[j, zs, u])
                        if h < 3 or (h == 3 and u == way):
                            hop(j, zs, u, way)
                if h < 4 or way == 1:
                    across(j, zs)

    def inputs_ready(j):
        arrived(ibuf.at[j, :, 0], sib_recv.at[j])

    def hand_over(src, parity, s):
        i = 2 * parity + x_hi
        for h in range(2):
            send(src, ebuf.at[x_lo, i, s], x_send.at[h], e_recv.at[x_lo, i, s], device(x_lo=1 - x_lo, x_hi=h))

    def errors_first(s):
        rows = err_ref.at[pl.ds(256 * s, 256)]
        i = 2 * odd + x_hi

        @pl.when(same)
        def _():
            pltpu.make_async_copy(rows, ebuf.at[x_lo, i, s], e_recv.at[x_lo, i, s]).start()
            send(rows, ebuf.at[x_lo, i, s], d_send, e_recv.at[x_lo, i, s], device(x_hi=1 - x_hi))

        @pl.when(other)
        def _():
            send(rows, rbuf.at[odd, s], y_send.at[0], r_recv.at[odd, s], pair)
            send(rows, rbuf.at[odd, s], y_send.at[1], r_recv.at[odd, s], beside)
            hand_over(rows, odd, s)

    def round_y(k, s):
        i = 2 * near + (x_hi if k == 0 else 1 - x_hi)
        slot, sem = ebuf.at[x_lo, i, s], e_recv.at[x_lo, i, s]
        arrived(slot, sem)
        send(slot, slot, y_send.at[0], sem, pair)

        @pl.when(same)
        def _():
            send(slot, slot, y_send.at[1], sem, beside)

    def passing(s):
        slot, sem = rbuf.at[1 - odd, s], r_recv.at[1 - odd, s]
        arrived(slot, sem)

        @pl.when(same)
        def _():
            send(slot, slot, y_send.at[0], sem, pair)

        hand_over(slot, 1 - odd, s)

    def passing_last(s):
        @pl.when(same)
        def _():
            arrived(rbuf.at[odd, s], r_recv.at[odd, s])
            hand_over(rbuf.at[odd, s], odd, s)

    def errors_ready(a, parity):
        for h in range(2):
            for s in range(4):
                arrived(ebuf.at[a, 2 * parity + h, s], e_recv.at[a, 2 * parity + h, s])

    def product(j, a):
        return lax.dot_general(
            ibuf[j].reshape(4096, 256), ebuf[a].reshape(4096, 256), (((0,), (0,)), ((), ())),
            preferred_element_type=jnp.float32,
        )

    def partial_sums(j):
        psend[j] = product(j, 1 - x_lo)
        send(psend.at[j], prec.at[j], rs_send.at[j], rs_recv.at[j], device(x_lo=1 - x_lo))

    for s in range(4):
        errors_first(s)
        if s < 2:
            inputs_first(s)

    def errors_steps(*steps):
        for f, *at in steps:
            f(*at)

    columns = pl.ds(pl.multiple_of((row % 4) * 256, 256), 256)

    def whole_sums(j):
        total = product(j, x_lo)
        arrived(prec.at[j], rs_recv.at[j])
        gt[j] = (total + prec[j]).reshape(32, 8, 256)

        @pl.loop(0, 32)
        def _(n):
            step = n // 4
            to_z = (z + jnp.where(step % 2 == 1, (step + 1) // 2, 8 - step // 2)) % 8
            to_row = ((n // 2) % 2) * 16 + to_z * 2 + n % 2
            src, dst = gt.at[j, to_row], gb_ref.at[col, pl.ds(8 * j, 8), columns]
            mine = at_home & (to_row == row)

            @pl.when(mine)
            def _():
                pltpu.make_async_copy(src, dst, p_recv).start()

            @pl.when(jnp.logical_not(mine))
            def _():
                send(src, dst, p_send, p_recv, (to_row, owner_col))

    early, late = (0, 1), (2, 3)
    errors_steps((round_y, 0, 0))
    inputs_step(early, 1)
    errors_steps((passing, 0), (passing, 1))
    inputs_step(early, 2)
    errors_steps((round_y, 0, 1), (passing, 2), (passing, 3))
    for j in late:
        own_inputs(j)
        inputs_first(j)
    inputs_step(early, 3)
    errors_steps((round_y, 0, 2), (round_y, 0, 3), (passing_last, 0), (passing_last, 1))
    inputs_step(early, 4)
    errors_steps((passing_last, 2), (passing_last, 3), (round_y, 1, 0))
    inputs_step(late, 1)
    errors_steps((round_y, 1, 1))
    for j in early:
        inputs_ready(j)
    for parity in range(2):
        errors_ready(1 - x_lo, parity)

    @pl.loop(0, 2)
    def _(j):
        partial_sums(j)

    inputs_step(late, 2)
    errors_steps((round_y, 1, 2), (round_y, 1, 3))
    inputs_step(late, 3)
    errors_ready(x_lo, 1 - near)
    whole_sums(0)
    inputs_step(late, 4)
    for j in late:
        inputs_ready(j)

    @pl.loop(2, 4)
    def _(j):
        partial_sums(j)

    @pl.loop(1, 4)
    def _(j):
        whole_sums(j)

    for t in range(8):
        units = jnp.concatenate([gt[j, 4 * t + a] for a in range(4) for j in range(4)], axis=0)
        gw_ref[:, 128 * t : 128 * t + 128] = units.T

    sent(ibuf.at[0, 0:7], i_send.at[0])
    sent(ibuf.at[0, 0:7], i_send.at[1])
    for j in range(4):
        sent(ibuf.at[j, :, 0], sib_send.at[j])
        sent(psend.at[j], rs_send.at[j])
    for h in range(2):
        sent(rbuf, x_send.at[h])
    sent(ebuf.at[0, 0:3], y_send.at[0])

    @pl.when(same)
    def _():
        sent(rbuf, y_send.at[1])
        sent(rbuf.at[0], d_send)

    @pl.when(other)
    def _():
        sent(rbuf.at[0], y_send.at[1])

    @pl.when(at_home)
    def _():
        sent(gt.at[:, 0:31], p_send)

    @pl.when(jnp.logical_not(at_home))
    def _():
        sent(gt, p_send)

    arrived(gb_ref, p_recv)


def gradients(errors, inputs):
    dma = pltpu.SemaphoreType.DMA
    hbm = pl.BlockSpec(memory_space=pltpu.HBM)
    vmem = pl.BlockSpec(memory_space=pltpu.VMEM)
    return pl.pallas_call(
        gradient_kernel,
        out_shape=(
            jax.ShapeDtypeStruct((256, 1024), jnp.float32),
            jax.ShapeDtypeStruct((8, 32, 1024), jnp.float32),
        ),
        in_specs=[hbm, vmem],
        out_specs=(vmem, vmem),
        scratch_shapes=[
            pltpu.VMEM((4, 8, 2, 256, 256), jnp.bfloat16),
            pltpu.VMEM((2, 4, 4, 256, 256), jnp.bfloat16),
            pltpu.VMEM((2, 4, 256, 256), jnp.bfloat16),
            pltpu.VMEM((4, 32, 8, 256), jnp.float32),
            pltpu.VMEM((4, 256, 256), jnp.float32),
            pltpu.VMEM((4, 256, 256), jnp.float32),
            dma((4, 8, 2)), dma((2,)), dma((4,)), dma((4,)),
            dma((2, 4, 4)), dma((2, 4)), dma, dma((2,)), dma((2,)),
            dma((4,)), dma((4,)), dma, dma,
        ],
        compiler_params=pltpu.CompilerParams(
            collective_id=0, has_side_effects=True, vmem_limit_bytes=32 << 20
        ),
        cost_estimate=pl.CostEstimate(flops=1 << 36, bytes_accessed=1 << 27, transcendentals=0),
        name="gradients",
    )(errors, inputs)


def shards(
    errors,
    inputs,
    weight,
    weight_moment_one,
    weight_moment_two,
    feedback,
    feedback_moment_one,
    feedback_moment_two,
):
    gradient, flipped = gradients(errors, inputs)
    return adam_update(weight, weight_moment_one, weight_moment_two, gradient) + adam_update(
        feedback, feedback_moment_one, feedback_moment_two, flipped
    )


def solution(mesh):
    whole, parts = P("row", "col"), P(None, "row", "col")
    return jax.shard_map(
        shards,
        mesh=mesh,
        in_specs=(P("col", "row"), whole, whole, whole, whole, parts, parts, parts),
        out_specs=(whole,) * 4 + (parts,) * 4,
        check_vma=False,
    )
```

```python
import jax
import jax.numpy as jnp
from jax import lax
from jax.experimental import pallas as pl
from jax.experimental.pallas import tpu as pltpu
from jax.sharding import PartitionSpec as P

beta_one = 0.9
beta_two = 0.999
learn_rate = 0.02
decay_rate = 0.1
epsilon = 1e-08
bias_one = 1.0
bias_two = 0.63230458

MESH = pl.DeviceIdType.MESH


def adam_update(master, moment_one, moment_two, gradient):
    first_new = beta_one * moment_one.astype(jnp.float32) + (1.0 - beta_one) * gradient
    second_new = beta_two * moment_two.astype(jnp.float32) + (1.0 - beta_two) * gradient * gradient
    update = first_new / bias_one / (jnp.sqrt(second_new / bias_two) + epsilon)
    master_new = master * (1.0 - learn_rate * decay_rate) - learn_rate * update
    return (
        master_new,
        first_new.astype(jnp.bfloat16),
        second_new.astype(jnp.bfloat16),
        master_new.astype(jnp.bfloat16),
    )


def update_kernel(
    err_ref, inp_hbm, *refs,
):
    (w_in, b_in), (w_out, b_out), (w_old, b_old) = ((refs[k : k + n], refs[k + n : k + 2 * n]) for k, n in ((0, 3), (6, 4), (14, 3)))
    (
    inp_ref, gb_ref, load, ibuf, ebuf, rbuf, gt, psend, prec,
    i_recv, i_send, sib_recv, sib_send, e_recv, r_recv, d_send, x_send, y_send, rs_recv, rs_send, p_recv, p_send,
    ) = refs[20:]
    row, col = lax.axis_index("row"), lax.axis_index("col")
    x_lo, z, core = row // 16, (row // 2) % 8, row % 2
    y, x_hi = col // 2, col % 2
    same = x_lo == y // 2
    other = jnp.logical_not(same)
    odd = y % 2
    near = jnp.where(same, odd, 1 - odd)
    pair_y, beside_y = y + 1 - 2 * odd, (y + 2 * odd + 3) % 4
    owner_col = row // 4
    at_home = owner_col == col

    def device(x_lo=x_lo, x_hi=x_hi, y=y, z=z, core=core):
        return (x_lo * 16 + z * 2 + core, y * 2 + x_hi)

    pair, beside, sibling = device(y=pair_y), device(y=beside_y), device(core=1 - core)

    def send(src, dst, send_sem, recv_sem, to):
        pltpu.make_async_remote_copy(
            src_ref=src, dst_ref=dst, send_sem=send_sem, recv_sem=recv_sem, device_id=to, device_id_type=MESH
        ).start()

    def arrived(ref, sem):
        pltpu.make_async_copy(ref, ref, sem).wait()

    def sent(ref, sem):
        pltpu.make_async_remote_copy(
            src_ref=ref, dst_ref=ref, send_sem=sem, recv_sem=sem, device_id=sibling, device_id_type=MESH
        ).wait_send()

    pltpu.make_async_copy(inp_hbm, inp_ref, load.at[6]).start()
    for k, (src, dst) in enumerate(zip((*w_in, *b_in), (*w_old, *b_old))):
        pltpu.make_async_copy(src, dst, load.at[k]).start()

    def own_inputs(j):
        unit = lax.broadcasted_iota(jnp.int32, (1024, 256), 0)
        place = lax.broadcasted_iota(jnp.int32, (1024, 256), 1)
        select = jnp.where(unit == (place // 8) * 32 + 8 * j + place % 8, 1.0, 0.0).astype(jnp.bfloat16)
        ibuf[j, z, core] = jnp.dot(inp_ref[...], select, preferred_element_type=jnp.float32).astype(jnp.bfloat16)

    barrier = pltpu.get_barrier_semaphore()

    def greet(to):
        pl.semaphore_signal(barrier, inc=1, device_id=to, device_id_type=MESH)

    greet(device(z=(z + 1) % 8))
    greet(device(z=(z + 7) % 8))
    greet(sibling)
    greet(pair)
    greet(beside)
    for h in range(2):
        greet(device(x_lo=1 - x_lo, x_hi=h))

    @pl.when(same)
    def _():
        greet(device(x_hi=1 - x_hi))

    @pl.loop(0, 32)
    def _(n):
        @pl.when(jnp.logical_not(at_home & (4 * col + n // 8 == row) & (n % 8 == col)))
        def _():
            greet((4 * col + n // 8, n % 8))

    arrived(inp_ref, load.at[6])
    own_inputs(0)
    own_inputs(1)
    pl.semaphore_wait(barrier, 39 + jnp.where(same, 1, 0) - jnp.where(at_home, 1, 0))

    def hop(j, zs, way, rows, sem):
        s = ibuf.at[j, zs, core, rows]
        send(s, s, i_send.at[way], i_recv.at[j, zs, sem], device(z=(z + (1, 7)[way]) % 8))

    def inputs_first(j):
        for way in range(2):
            hop(j, z, way, pl.ds(0, 256), 0)

    def inputs_step(j, h):
        for way in range(2):
            zs = (z + (8 - h, h)[way]) % 8
            if h < 4:
                arrived(ibuf.at[j, zs, core], i_recv.at[j, zs, 0])
            else:
                arrived(ibuf.at[j, zs, core, pl.ds(128 * way, 128)], i_recv.at[j, zs, way])
            if h < 3:
                hop(j, zs, way, pl.ds(0, 256), 0)
            elif h == 3:
                hop(j, zs, way, pl.ds(128 * way, 128), way)

    def across(j, count, h):
        for zs in ((z + 8 - h) % 8, (z + h) % 8)[0 if h % 4 else 1 :]:
            s = ibuf.at[pl.ds(j, count), zs, core]
            send(s, s, sib_send.at[j], sib_recv.at[j], sibling)

    def inputs_ready(j, count):
        arrived(ibuf.at[pl.ds(j, count), :, 0], sib_recv.at[j])

    def hand_over(src, parity, s):
        i = 2 * parity + x_hi
        for h in range(2):
            send(src, ebuf.at[x_lo, i, s], x_send.at[h], e_recv.at[x_lo, i, s], device(x_lo=1 - x_lo, x_hi=h))

    def errors_first(s):
        rows = err_ref.at[pl.ds(256 * s, 256)]
        i = 2 * odd + x_hi

        @pl.when(same)
        def _():
            pltpu.make_async_copy(rows, ebuf.at[x_lo, i, s], e_recv.at[x_lo, i, s]).start()
            send(rows, ebuf.at[x_lo, i, s], d_send, e_recv.at[x_lo, i, s], device(x_hi=1 - x_hi))

        @pl.when(other)
        def _():
            send(rows, rbuf.at[odd, s], y_send.at[0], r_recv.at[odd, s], pair)
            send(rows, rbuf.at[odd, s], y_send.at[1], r_recv.at[odd, s], beside)
            hand_over(rows, odd, s)

    def round_y(k, s):
        i = 2 * near + (x_hi if k == 0 else 1 - x_hi)
        slot, sem = ebuf.at[x_lo, i, s], e_recv.at[x_lo, i, s]
        arrived(slot, sem)
        send(slot, slot, y_send.at[0], sem, pair)

        @pl.when(same)
        def _():
            send(slot, slot, y_send.at[1], sem, beside)

    def passing(s):
        slot, sem = rbuf.at[1 - odd, s], r_recv.at[1 - odd, s]
        arrived(slot, sem)

        @pl.when(same)
        def _():
            send(slot, slot, y_send.at[0], sem, pair)

        hand_over(slot, 1 - odd, s)

    def passing_last(s):
        @pl.when(same)
        def _():
            arrived(rbuf.at[odd, s], r_recv.at[odd, s])
            hand_over(rbuf.at[odd, s], odd, s)

    def errors_ready(a, parity):
        for h in range(2):
            for s in range(4):
                arrived(ebuf.at[a, 2 * parity + h, s], e_recv.at[a, 2 * parity + h, s])

    def product(j, a):
        return lax.dot_general(
            ibuf[j].reshape(4096, 256), ebuf[a].reshape(4096, 256), (((0,), (0,)), ((), ())),
            preferred_element_type=jnp.float32,
        )

    def partial_sums(j):
        psend[j] = product(j, 1 - x_lo)
        send(psend.at[j], prec.at[j], rs_send.at[j], rs_recv.at[j], device(x_lo=1 - x_lo))

    for s in range(4):
        errors_first(s)
        if s < 2:
            inputs_first(s)

    def errors_steps(*steps):
        for f, *at in steps:
            f(*at)

    columns = pl.ds(pl.multiple_of((row % 4) * 256, 256), 256)

    def whole_sums(j):
        total = product(j, x_lo)
        arrived(prec.at[j], rs_recv.at[j])
        gt[:, pl.ds(pl.multiple_of(8 * j, 8), 8)] = (total + prec[j]).reshape(32, 8, 256)

    def to_owners(j, count, group):
        @pl.loop(0, 32)
        def _(n):
            step = n // 4
            to_z = (z + jnp.where(step % 2 == 1, (step + 1) // 2, 8 - step // 2)) % 8
            to_row = ((n // 2) % 2) * 16 + to_z * 2 + n % 2
            src = gt.at[to_row, pl.ds(8 * j, 8 * count)]
            dst = gb_ref.at[col, pl.ds(8 * j, 8 * count), columns]
            mine = at_home & (to_row == row)

            @pl.when(mine)
            def _():
                pltpu.make_async_copy(src, dst, p_recv.at[group]).start()

            @pl.when(jnp.logical_not(mine))
            def _():
                send(src, dst, p_send, p_recv.at[group], (to_row, owner_col))

    errors_steps((round_y, 0, 0))
    across(0, 2, 0)
    inputs_step(0, 1)
    inputs_step(1, 1)
    across(0, 2, 1)
    errors_steps((passing, 0), (passing, 1))
    inputs_step(0, 2)
    inputs_step(1, 2)
    across(0, 2, 2)
    own_inputs(2)
    inputs_first(2)
    errors_steps((round_y, 0, 1), (passing, 2), (passing, 3))
    inputs_step(0, 3)
    inputs_step(1, 3)
    across(0, 2, 3)
    inputs_step(2, 1)
    across(2, 1, 0)
    across(2, 1, 1)
    own_inputs(3)
    inputs_first(3)
    errors_steps((round_y, 0, 2), (round_y, 0, 3), (passing_last, 0), (passing_last, 1))
    inputs_step(0, 4)
    inputs_step(1, 4)
    across(0, 2, 4)
    errors_steps((passing_last, 2), (passing_last, 3), (round_y, 1, 0))
    inputs_step(2, 2)
    across(2, 1, 2)
    inputs_step(3, 1)
    across(3, 1, 0)
    across(3, 1, 1)
    errors_steps((round_y, 1, 1))
    inputs_step(2, 3)
    across(2, 1, 3)
    inputs_ready(0, 2)
    for parity in range(2):
        errors_ready(1 - x_lo, parity)

    @pl.loop(0, 2)
    def _(j):
        partial_sums(j)

    inputs_step(3, 2)
    across(3, 1, 2)
    errors_steps((round_y, 1, 2), (round_y, 1, 3))
    inputs_step(2, 4)
    across(2, 1, 4)
    inputs_step(3, 3)
    across(3, 1, 3)
    inputs_ready(2, 1)
    partial_sums(2)
    errors_ready(x_lo, 1 - near)

    @pl.loop(0, 2)
    def _(j):
        whole_sums(j)

    to_owners(0, 2, 0)
    inputs_step(3, 4)
    across(3, 1, 4)
    inputs_ready(3, 1)
    partial_sums(3)

    @pl.loop(2, 4)
    def _(j):
        whole_sums(j)
        to_owners(j, 1, j - 1)

    for k, ref in enumerate((*w_old, *b_old)):
        arrived(ref, load.at[k])

    def update(old, out, at, gradient):
        for ref, new in zip(out, adam_update(*(ref[at] for ref in old), gradient)):
            ref[at] = new

    @pl.loop(0, 8)
    def _(t):
        units = pl.ds(pl.multiple_of(128 * t, 128), 128)
        update(w_old, w_out, (slice(None), units), gt[pl.ds(4 * t, 4)].reshape(128, 256).T)

    def update_feedback(first):
        @pl.loop(0, 8)
        def _(g):
            at = (g, pl.ds(first, 16))
            update(b_old, b_out, at, gb_ref[at])

    arrived(gb_ref.at[:, pl.ds(0, 16)], p_recv.at[0])
    update_feedback(0)
    for k in (1, 2):
        arrived(gb_ref.at[:, pl.ds(8 + 8 * k, 8)], p_recv.at[k])
    update_feedback(16)

    sent(ibuf.at[0, 0:7], i_send.at[0])
    sent(ibuf.at[0, 0:7], i_send.at[1])
    for j, count in ((0, 2), (2, 1), (3, 1)):
        sent(ibuf.at[pl.ds(j, count), :, 0], sib_send.at[j])
    for j in range(4):
        sent(psend.at[j], rs_send.at[j])
    for h in range(2):
        sent(rbuf, x_send.at[h])
    sent(ebuf.at[0, 0:3], y_send.at[0])

    @pl.when(same)
    def _():
        sent(rbuf, y_send.at[1])
        sent(rbuf.at[0], d_send)

    @pl.when(other)
    def _():
        sent(rbuf.at[0], y_send.at[1])

    @pl.when(at_home)
    def _():
        sent(gt.at[0:31], p_send)

    @pl.when(jnp.logical_not(at_home))
    def _():
        sent(gt, p_send)


def shards(errors, inputs, *states):
    dma = pltpu.SemaphoreType.DMA
    old = [pltpu.VMEM(state.shape, state.dtype) for state in states]
    new = [
        jax.ShapeDtypeStruct(states[k].shape, dtype)
        for k in (0, 3)
        for dtype in (jnp.float32, jnp.bfloat16, jnp.bfloat16, jnp.bfloat16)
    ]
    return pl.pallas_call(
        update_kernel,
        out_shape=new,
        in_specs=[pl.BlockSpec(memory_space=pltpu.HBM)] * 8,
        out_specs=[pl.BlockSpec(memory_space=pltpu.VMEM)] * 8,
        scratch_shapes=old + [
            pltpu.VMEM((256, 1024), jnp.bfloat16),
            pltpu.VMEM((8, 32, 1024), jnp.float32),
            dma((7,)),
            pltpu.VMEM((4, 8, 2, 256, 256), jnp.bfloat16),
            pltpu.VMEM((2, 4, 4, 256, 256), jnp.bfloat16),
            pltpu.VMEM((2, 4, 256, 256), jnp.bfloat16),
            pltpu.VMEM((32, 32, 256), jnp.float32),
            pltpu.VMEM((4, 256, 256), jnp.float32),
            pltpu.VMEM((4, 256, 256), jnp.float32),
            dma((4, 8, 2)), dma((2,)), dma((4,)), dma((4,)),
            dma((2, 4, 4)), dma((2, 4)), dma, dma((2,)), dma((2,)),
            dma((4,)), dma((4,)), dma((3,)), dma,
        ],
        compiler_params=pltpu.CompilerParams(
            collective_id=0, has_side_effects=True, vmem_limit_bytes=36 << 20
        ),
        cost_estimate=pl.CostEstimate(flops=1 << 36, bytes_accessed=1 << 27, transcendentals=0),
        name="gradients",
    )(*(pltpu.with_memory_space_constraint(array, pltpu.HBM) for array in (errors, inputs, *states)))


def solution(mesh):
    whole, parts = P("row", "col"), P(None, "row", "col")
    return jax.shard_map(
        shards,
        mesh=mesh,
        in_specs=(P("col", "row"), whole, whole, whole, whole, parts, parts, parts),
        out_specs=(whole,) * 4 + (parts,) * 4,
        check_vma=False,
    )
```

```python
import jax
import jax.numpy as jnp
from jax import lax
from jax.experimental import pallas as pl
from jax.experimental.pallas import tpu as pltpu
from jax.sharding import PartitionSpec as P

beta_one = 0.9
beta_two = 0.999
learn_rate = 0.02
decay_rate = 0.1
epsilon = 1e-08
bias_one = 1.0
bias_two = 0.63230458

MESH = pl.DeviceIdType.MESH


def adam_update(master, moment_one, moment_two, gradient):
    first_new = beta_one * moment_one.astype(jnp.float32) + (1.0 - beta_one) * gradient
    second_new = beta_two * moment_two.astype(jnp.float32) + (1.0 - beta_two) * gradient * gradient
    update = first_new / bias_one / (jnp.sqrt(second_new / bias_two) + epsilon)
    master_new = master * (1.0 - learn_rate * decay_rate) - learn_rate * update
    return (
        master_new,
        first_new.astype(jnp.bfloat16),
        second_new.astype(jnp.bfloat16),
        master_new.astype(jnp.bfloat16),
    )


def update_kernel(
    err_ref, inp_hbm, *refs,
):
    (w_in, b_in), (w_out, b_out), (w_old, b_old) = ((refs[k : k + n], refs[k + n : k + 2 * n]) for k, n in ((0, 3), (6, 4), (14, 3)))
    (
    inp_ref, gb_ref, load, ibuf, ebuf, rbuf, gt, psend, prec,
    i_recv, i_send, sib_recv, sib_send, e_recv, r_recv, d_send, x_send, y_send, rs_recv, rs_send, p_recv, p_send,
    ) = refs[20:]
    row, col = lax.axis_index("row"), lax.axis_index("col")
    x_lo, z, core = row // 16, (row // 2) % 8, row % 2
    y, x_hi = col // 2, col % 2
    same = x_lo == y // 2
    other = jnp.logical_not(same)
    odd = y % 2
    near = jnp.where(same, odd, 1 - odd)
    pair_y, beside_y = y + 1 - 2 * odd, (y + 2 * odd + 3) % 4
    owner_col = row // 4
    at_home = owner_col == col

    def device(x_lo=x_lo, x_hi=x_hi, y=y, z=z, core=core):
        return (x_lo * 16 + z * 2 + core, y * 2 + x_hi)

    pair, beside, sibling = device(y=pair_y), device(y=beside_y), device(core=1 - core)

    def send(src, dst, send_sem, recv_sem, to):
        pltpu.make_async_remote_copy(
            src_ref=src, dst_ref=dst, send_sem=send_sem, recv_sem=recv_sem, device_id=to, device_id_type=MESH
        ).start()

    def arrived(ref, sem):
        pltpu.make_async_copy(ref, ref, sem).wait()

    def sent(ref, sem):
        pltpu.make_async_remote_copy(
            src_ref=ref, dst_ref=ref, send_sem=sem, recv_sem=sem, device_id=sibling, device_id_type=MESH
        ).wait_send()

    pltpu.make_async_copy(inp_hbm, inp_ref, load.at[6]).start()
    for k, (src, dst) in enumerate(zip((*w_in, *b_in), (*w_old, *b_old))):
        pltpu.make_async_copy(src, dst, load.at[k]).start()

    def own_inputs(j):
        unit = lax.broadcasted_iota(jnp.int32, (1024, 256), 0)
        place = lax.broadcasted_iota(jnp.int32, (1024, 256), 1)
        select = jnp.where(unit == (place // 8) * 32 + 8 * j + place % 8, 1.0, 0.0).astype(jnp.bfloat16)
        ibuf[j, z, core] = jnp.dot(inp_ref[...], select, preferred_element_type=jnp.float32).astype(jnp.bfloat16)

    barrier = pltpu.get_barrier_semaphore()

    def greet(to):
        pl.semaphore_signal(barrier, inc=1, device_id=to, device_id_type=MESH)

    greet(device(z=(z + 1) % 8))
    greet(device(z=(z + 7) % 8))
    greet(sibling)
    greet(pair)
    greet(beside)
    for h in range(2):
        greet(device(x_lo=1 - x_lo, x_hi=h))

    @pl.when(same)
    def _():
        greet(device(x_hi=1 - x_hi))

    @pl.loop(0, 32)
    def _(n):
        @pl.when(jnp.logical_not(at_home & (4 * col + n // 8 == row) & (n % 8 == col)))
        def _():
            greet((4 * col + n // 8, n % 8))

    arrived(inp_ref, load.at[6])
    own_inputs(0)
    own_inputs(1)
    pl.semaphore_wait(barrier, 39 + jnp.where(same, 1, 0) - jnp.where(at_home, 1, 0))

    def hop(j, zs, way, rows, sem):
        s = ibuf.at[j, zs, core, rows]
        send(s, s, i_send.at[way], i_recv.at[j, zs, sem], device(z=(z + (1, 7)[way]) % 8))

    def inputs_first(j):
        for way in range(2):
            hop(j, z, way, pl.ds(0, 256), 0)

    def inputs_step(j, h):
        for way in range(2):
            zs = (z + (8 - h, h)[way]) % 8
            if h < 4:
                arrived(ibuf.at[j, zs, core], i_recv.at[j, zs, 0])
            else:
                arrived(ibuf.at[j, zs, core, pl.ds(128 * way, 128)], i_recv.at[j, zs, way])
            if h < 3:
                hop(j, zs, way, pl.ds(0, 256), 0)
            elif h == 3:
                hop(j, zs, way, pl.ds(128 * way, 128), way)

    def across(j, count, h):
        for zs in ((z + 8 - h) % 8, (z + h) % 8)[0 if h % 4 else 1 :]:
            s = ibuf.at[pl.ds(j, count), zs, core]
            send(s, s, sib_send.at[j], sib_recv.at[j], sibling)

    def inputs_ready(j, count):
        arrived(ibuf.at[pl.ds(j, count), :, 0], sib_recv.at[j])

    def hand_over(src, parity, s):
        i = 2 * parity + x_hi
        for h in range(2):
            send(src, ebuf.at[x_lo, i, s], x_send.at[h], e_recv.at[x_lo, i, s], device(x_lo=1 - x_lo, x_hi=h))

    def errors_first(s):
        rows = err_ref.at[pl.ds(256 * s, 256)]
        i = 2 * odd + x_hi

        @pl.when(same)
        def _():
            pltpu.make_async_copy(rows, ebuf.at[x_lo, i, s], e_recv.at[x_lo, i, s]).start()
            send(rows, ebuf.at[x_lo, i, s], d_send, e_recv.at[x_lo, i, s], device(x_hi=1 - x_hi))

        @pl.when(other)
        def _():
            send(rows, rbuf.at[odd, s], y_send.at[0], r_recv.at[odd, s], pair)
            send(rows, rbuf.at[odd, s], y_send.at[1], r_recv.at[odd, s], beside)
            hand_over(rows, odd, s)

    def round_y(k, s):
        i = 2 * near + (x_hi if k == 0 else 1 - x_hi)
        slot, sem = ebuf.at[x_lo, i, s], e_recv.at[x_lo, i, s]
        arrived(slot, sem)
        send(slot, slot, y_send.at[0], sem, pair)

        @pl.when(same)
        def _():
            send(slot, slot, y_send.at[1], sem, beside)

    def passing(s):
        slot, sem = rbuf.at[1 - odd, s], r_recv.at[1 - odd, s]
        arrived(slot, sem)

        @pl.when(same)
        def _():
            send(slot, slot, y_send.at[0], sem, pair)

        hand_over(slot, 1 - odd, s)

    def passing_last(s):
        @pl.when(same)
        def _():
            arrived(rbuf.at[odd, s], r_recv.at[odd, s])
            hand_over(rbuf.at[odd, s], odd, s)

    def errors_ready(a, parity):
        for h in range(2):
            for s in range(4):
                arrived(ebuf.at[a, 2 * parity + h, s], e_recv.at[a, 2 * parity + h, s])

    def product(j, a):
        return lax.dot_general(
            ibuf[j].reshape(4096, 256), ebuf[a].reshape(4096, 256), (((0,), (0,)), ((), ())),
            preferred_element_type=jnp.float32,
        )

    def partial_sums(j):
        psend[j] = product(j, 1 - x_lo)
        send(psend.at[j], prec.at[j], rs_send.at[j], rs_recv.at[j], device(x_lo=1 - x_lo))

    for s in range(4):
        errors_first(s)
        if s < 2:
            inputs_first(s)

    def errors_steps(*steps):
        for f, *at in steps:
            f(*at)

    columns = pl.ds(pl.multiple_of((row % 4) * 256, 256), 256)

    def whole_sums(j):
        total = product(j, x_lo)
        arrived(prec.at[j], rs_recv.at[j])
        gt[:, pl.ds(pl.multiple_of(8 * j, 8), 8)] = (total + prec[j]).reshape(32, 8, 256)

    def to_owners(j, count, group):
        @pl.loop(0, 32)
        def _(n):
            step = n // 4
            to_z = (z + jnp.where(step % 2 == 1, (step + 1) // 2, 8 - step // 2)) % 8
            to_row = ((n // 2) % 2) * 16 + to_z * 2 + n % 2
            src = gt.at[to_row, pl.ds(8 * j, 8 * count)]
            dst = gb_ref.at[col, pl.ds(8 * j, 8 * count), columns]
            mine = at_home & (to_row == row)

            @pl.when(mine)
            def _():
                pltpu.make_async_copy(src, dst, p_recv.at[group]).start()

            @pl.when(jnp.logical_not(mine))
            def _():
                send(src, dst, p_send, p_recv.at[group], (to_row, owner_col))

    errors_steps((round_y, 0, 0))
    across(0, 2, 0)
    inputs_step(0, 1)
    inputs_step(1, 1)
    across(0, 2, 1)
    errors_steps((passing, 0), (passing, 1))
    inputs_step(0, 2)
    inputs_step(1, 2)
    across(0, 2, 2)
    own_inputs(2)
    inputs_first(2)
    errors_steps((round_y, 0, 1), (passing, 2), (passing, 3))
    inputs_step(0, 3)
    inputs_step(1, 3)
    across(0, 2, 3)
    inputs_step(2, 1)
    across(2, 1, 0)
    across(2, 1, 1)
    own_inputs(3)
    inputs_first(3)
    errors_steps((round_y, 0, 2), (round_y, 0, 3), (passing_last, 0), (passing_last, 1))
    inputs_step(0, 4)
    inputs_step(1, 4)
    across(0, 2, 4)
    errors_steps((passing_last, 2), (passing_last, 3), (round_y, 1, 0))
    inputs_step(2, 2)
    across(2, 1, 2)
    inputs_step(3, 1)
    across(3, 1, 0)
    across(3, 1, 1)
    errors_steps((round_y, 1, 1))
    inputs_step(2, 3)
    across(2, 1, 3)
    inputs_ready(0, 2)
    for parity in range(2):
        errors_ready(1 - x_lo, parity)

    @pl.loop(0, 2)
    def _(j):
        partial_sums(j)

    inputs_step(3, 2)
    across(3, 1, 2)
    errors_steps((round_y, 1, 2), (round_y, 1, 3))
    inputs_step(2, 4)
    across(2, 1, 4)
    inputs_step(3, 3)
    across(3, 1, 3)
    inputs_ready(2, 1)
    partial_sums(2)
    errors_ready(x_lo, 1 - near)

    @pl.loop(0, 2)
    def _(j):
        whole_sums(j)

    to_owners(0, 2, 0)
    inputs_step(3, 4)
    across(3, 1, 4)
    inputs_ready(3, 1)
    partial_sums(3)

    @pl.loop(2, 4)
    def _(j):
        whole_sums(j)
        to_owners(j, 1, j - 1)

    for k, ref in enumerate((*w_old, *b_old)):
        arrived(ref, load.at[k])

    def update(old, out, at, gradient):
        for ref, new in zip(out, adam_update(*(ref[at] for ref in old), gradient)):
            ref[at] = new

    @pl.loop(0, 8)
    def _(t):
        units = pl.ds(pl.multiple_of(128 * t, 128), 128)
        update(w_old, w_out, (slice(None), units), gt[pl.ds(4 * t, 4)].reshape(128, 256).T)

    def update_feedback(first):
        @pl.loop(0, 8)
        def _(g):
            at = (g, pl.ds(first, 16))
            update(b_old, b_out, at, gb_ref[at])

    arrived(gb_ref.at[:, pl.ds(0, 16)], p_recv.at[0])
    update_feedback(0)
    for k in (1, 2):
        arrived(gb_ref.at[:, pl.ds(8 + 8 * k, 8)], p_recv.at[k])
    update_feedback(16)

    sent(ibuf.at[0, 0:7], i_send.at[0])
    sent(ibuf.at[0, 0:7], i_send.at[1])
    for j, count in ((0, 2), (2, 1), (3, 1)):
        sent(ibuf.at[pl.ds(j, count), :, 0], sib_send.at[j])
    for j in range(4):
        sent(psend.at[j], rs_send.at[j])
    for h in range(2):
        sent(rbuf, x_send.at[h])
    sent(ebuf.at[0, 0:3], y_send.at[0])

    @pl.when(same)
    def _():
        sent(rbuf, y_send.at[1])
        sent(rbuf.at[0], d_send)

    @pl.when(other)
    def _():
        sent(rbuf.at[0], y_send.at[1])

    @pl.when(at_home)
    def _():
        sent(gt.at[0:31], p_send)

    @pl.when(jnp.logical_not(at_home))
    def _():
        sent(gt, p_send)


def store_kernel(*refs):
    copies = [pltpu.make_async_copy(refs[k], refs[8 + k], refs[16].at[k]) for k in range(8)]
    for copy in copies:
        copy.start()
    for copy in copies:
        copy.wait()


def shards(errors, inputs, *states):
    dma = pltpu.SemaphoreType.DMA
    old = [pltpu.VMEM(state.shape, state.dtype) for state in states]
    new = [
        jax.ShapeDtypeStruct(states[k].shape, dtype)
        for k in (0, 3)
        for dtype in (jnp.float32, jnp.bfloat16, jnp.bfloat16, jnp.bfloat16)
    ]
    results = pl.pallas_call(
        update_kernel,
        out_shape=new,
        in_specs=[pl.BlockSpec(memory_space=pltpu.HBM)] * 8,
        out_specs=[pl.BlockSpec(memory_space=pltpu.VMEM)] * 8,
        scratch_shapes=old + [
            pltpu.VMEM((256, 1024), jnp.bfloat16),
            pltpu.VMEM((8, 32, 1024), jnp.float32),
            dma((7,)),
            pltpu.VMEM((4, 8, 2, 256, 256), jnp.bfloat16),
            pltpu.VMEM((2, 4, 4, 256, 256), jnp.bfloat16),
            pltpu.VMEM((2, 4, 256, 256), jnp.bfloat16),
            pltpu.VMEM((32, 32, 256), jnp.float32),
            pltpu.VMEM((4, 256, 256), jnp.float32),
            pltpu.VMEM((4, 256, 256), jnp.float32),
            dma((4, 8, 2)), dma((2,)), dma((4,)), dma((4,)),
            dma((2, 4, 4)), dma((2, 4)), dma, dma((2,)), dma((2,)),
            dma((4,)), dma((4,)), dma((3,)), dma,
        ],
        compiler_params=pltpu.CompilerParams(
            collective_id=0, has_side_effects=True, vmem_limit_bytes=36 << 20
        ),
        cost_estimate=pl.CostEstimate(flops=1 << 36, bytes_accessed=1 << 27, transcendentals=0),
        name="gradients",
    )(*(pltpu.with_memory_space_constraint(array, pltpu.HBM) for array in (errors, inputs, *states)))
    return pl.pallas_call(
        store_kernel,
        out_shape=new,
        in_specs=[pl.BlockSpec(memory_space=pltpu.VMEM)] * 8,
        out_specs=[pl.BlockSpec(memory_space=pltpu.HBM)] * 8,
        scratch_shapes=[dma((8,))],
        compiler_params=pltpu.CompilerParams(vmem_limit_bytes=8 << 20),
        name="store",
    )(*results)


def solution(mesh):
    whole, parts = P("row", "col"), P(None, "row", "col")
    return jax.shard_map(
        shards,
        mesh=mesh,
        in_specs=(P("col", "row"), whole, whole, whole, whole, parts, parts, parts),
        out_specs=(whole,) * 4 + (parts,) * 4,
        check_vma=False,
    )
```

```python
import jax
import jax.numpy as jnp
from jax import lax
from jax.experimental import pallas as pl
from jax.experimental.pallas import tpu as pltpu
from jax.sharding import PartitionSpec as P

beta_one = 0.9
beta_two = 0.999
learn_rate = 0.02
decay_rate = 0.1
epsilon = 1e-08
bias_one = 1.0
bias_two = 0.63230458

MESH = pl.DeviceIdType.MESH


def adam_update(master, moment_one, moment_two, gradient):
    first_new = beta_one * moment_one.astype(jnp.float32) + (1.0 - beta_one) * gradient
    second_new = beta_two * moment_two.astype(jnp.float32) + (1.0 - beta_two) * gradient * gradient
    update = first_new / bias_one / (jnp.sqrt(second_new / bias_two) + epsilon)
    master_new = master * (1.0 - learn_rate * decay_rate) - learn_rate * update
    return (
        master_new,
        first_new.astype(jnp.bfloat16),
        second_new.astype(jnp.bfloat16),
        master_new.astype(jnp.bfloat16),
    )


def update_kernel(
    err_ref, inp_hbm, *refs,
):
    (w_in, b_in), (w_out, b_out), (w_old, b_old) = ((refs[k : k + n], refs[k + n : k + 2 * n]) for k, n in ((0, 3), (6, 4), (14, 3)))
    (
    inp_ref, gb_ref, load, ibuf, ebuf, rbuf, gt, psend, prec,
    i_recv, i_send, sib_recv, sib_send, e_recv, r_recv, d_send, x_send, y_send, rs_recv, rs_send, p_recv, p_send,
    ) = refs[20:]
    row, col = lax.axis_index("row"), lax.axis_index("col")
    x_lo, z, core = row // 16, (row // 2) % 8, row % 2
    y, x_hi = col // 2, col % 2
    same = x_lo == y // 2
    other = jnp.logical_not(same)
    odd = y % 2
    near = jnp.where(same, odd, 1 - odd)
    pair_y, beside_y = y + 1 - 2 * odd, (y + 2 * odd + 3) % 4
    owner_col = row // 4
    at_home = owner_col == col

    def device(x_lo=x_lo, x_hi=x_hi, y=y, z=z, core=core):
        return (x_lo * 16 + z * 2 + core, y * 2 + x_hi)

    pair, beside, sibling = device(y=pair_y), device(y=beside_y), device(core=1 - core)

    def send(src, dst, send_sem, recv_sem, to):
        pltpu.make_async_remote_copy(
            src_ref=src, dst_ref=dst, send_sem=send_sem, recv_sem=recv_sem, device_id=to, device_id_type=MESH
        ).start()

    def arrived(ref, sem):
        pltpu.make_async_copy(ref, ref, sem).wait()

    def sent(ref, sem):
        pltpu.make_async_remote_copy(
            src_ref=ref, dst_ref=ref, send_sem=sem, recv_sem=sem, device_id=sibling, device_id_type=MESH
        ).wait_send()

    pltpu.make_async_copy(inp_hbm, inp_ref, load.at[6]).start()
    for k, (src, dst) in enumerate(zip((*w_in, *b_in), (*w_old, *b_old))):
        pltpu.make_async_copy(src, dst, load.at[k]).start()

    def own_inputs(j):
        unit = lax.broadcasted_iota(jnp.int32, (1024, 256), 0)
        place = lax.broadcasted_iota(jnp.int32, (1024, 256), 1)
        select = jnp.where(unit == (place // 8) * 32 + 8 * j + place % 8, 1.0, 0.0).astype(jnp.bfloat16)
        ibuf[j, z, core] = jnp.dot(inp_ref[...], select, preferred_element_type=jnp.float32).astype(jnp.bfloat16)

    barrier = pltpu.get_barrier_semaphore()

    def greet(to):
        pl.semaphore_signal(barrier, inc=1, device_id=to, device_id_type=MESH)

    greet(device(z=(z + 1) % 8))
    greet(device(z=(z + 7) % 8))
    greet(sibling)
    greet(pair)
    greet(beside)
    for h in range(2):
        greet(device(x_lo=1 - x_lo, x_hi=h))

    @pl.when(same)
    def _():
        greet(device(x_hi=1 - x_hi))

    @pl.loop(0, 32)
    def _(n):
        @pl.when(jnp.logical_not(at_home & (4 * col + n // 8 == row) & (n % 8 == col)))
        def _():
            greet((4 * col + n // 8, n % 8))

    arrived(inp_ref, load.at[6])
    own_inputs(0)
    own_inputs(1)
    pl.semaphore_wait(barrier, 39 + jnp.where(same, 1, 0) - jnp.where(at_home, 1, 0))

    def hop(j, zs, way, rows, sem):
        s = ibuf.at[j, zs, core, rows]
        send(s, s, i_send.at[way], i_recv.at[j, zs, sem], device(z=(z + (1, 7)[way]) % 8))

    def inputs_first(j):
        for way in range(2):
            hop(j, z, way, pl.ds(0, 256), 0)

    def inputs_step(j, h):
        for way in range(2):
            zs = (z + (8 - h, h)[way]) % 8
            if h < 4:
                arrived(ibuf.at[j, zs, core], i_recv.at[j, zs, 0])
            else:
                arrived(ibuf.at[j, zs, core, pl.ds(128 * way, 128)], i_recv.at[j, zs, way])
            if h < 3:
                hop(j, zs, way, pl.ds(0, 256), 0)
            elif h == 3:
                hop(j, zs, way, pl.ds(128 * way, 128), way)

    def across(j, count, h):
        for zs in ((z + 8 - h) % 8, (z + h) % 8)[0 if h % 4 else 1 :]:
            s = ibuf.at[pl.ds(j, count), zs, core]
            send(s, s, sib_send.at[j], sib_recv.at[j], sibling)

    def inputs_ready(j, count):
        arrived(ibuf.at[pl.ds(j, count), :, 0], sib_recv.at[j])

    def hand_over(src, parity, s):
        i = 2 * parity + x_hi
        for h in range(2):
            send(src, ebuf.at[x_lo, i, s], x_send.at[h], e_recv.at[x_lo, i, s], device(x_lo=1 - x_lo, x_hi=h))

    def errors_first(s):
        rows = err_ref.at[pl.ds(256 * s, 256)]
        i = 2 * odd + x_hi

        @pl.when(same)
        def _():
            pltpu.make_async_copy(rows, ebuf.at[x_lo, i, s], e_recv.at[x_lo, i, s]).start()
            send(rows, ebuf.at[x_lo, i, s], d_send, e_recv.at[x_lo, i, s], device(x_hi=1 - x_hi))

        @pl.when(other)
        def _():
            send(rows, rbuf.at[odd, s], y_send.at[0], r_recv.at[odd, s], pair)
            send(rows, rbuf.at[odd, s], y_send.at[1], r_recv.at[odd, s], beside)
            hand_over(rows, odd, s)

    def round_y(k, s):
        i = 2 * near + (x_hi if k == 0 else 1 - x_hi)
        slot, sem = ebuf.at[x_lo, i, s], e_recv.at[x_lo, i, s]
        arrived(slot, sem)
        send(slot, slot, y_send.at[0], sem, pair)

        @pl.when(same)
        def _():
            send(slot, slot, y_send.at[1], sem, beside)

    def passing(s):
        slot, sem = rbuf.at[1 - odd, s], r_recv.at[1 - odd, s]
        arrived(slot, sem)

        @pl.when(same)
        def _():
            send(slot, slot, y_send.at[0], sem, pair)

        hand_over(slot, 1 - odd, s)

    def passing_last(s):
        @pl.when(same)
        def _():
            arrived(rbuf.at[odd, s], r_recv.at[odd, s])
            hand_over(rbuf.at[odd, s], odd, s)

    def errors_ready(a, parity):
        for h in range(2):
            for s in range(4):
                arrived(ebuf.at[a, 2 * parity + h, s], e_recv.at[a, 2 * parity + h, s])

    def product(j, a):
        return lax.dot_general(
            ibuf[j].reshape(4096, 256), ebuf[a].reshape(4096, 256), (((0,), (0,)), ((), ())),
            preferred_element_type=jnp.float32,
        )

    def partial_sums(j):
        psend[j] = product(j, 1 - x_lo)
        send(psend.at[j], prec.at[j], rs_send.at[j], rs_recv.at[j], device(x_lo=1 - x_lo))

    for s in range(4):
        errors_first(s)
        if s < 2:
            inputs_first(s)

    def errors_steps(*steps):
        for f, *at in steps:
            f(*at)

    columns = pl.ds(pl.multiple_of((row % 4) * 256, 256), 256)

    def whole_sums(j):
        total = product(j, x_lo)
        arrived(prec.at[j], rs_recv.at[j])
        gt[:, pl.ds(pl.multiple_of(8 * j, 8), 8)] = (total + prec[j]).reshape(32, 8, 256)

    def to_owners(j, count, group):
        @pl.loop(0, 32)
        def _(n):
            step = n // 4
            to_z = (z + jnp.where(step % 2 == 1, (step + 1) // 2, 8 - step // 2)) % 8
            to_row = ((n // 2) % 2) * 16 + to_z * 2 + n % 2
            src = gt.at[to_row, pl.ds(8 * j, 8 * count)]
            dst = gb_ref.at[col, pl.ds(8 * j, 8 * count), columns]
            mine = at_home & (to_row == row)

            @pl.when(mine)
            def _():
                pltpu.make_async_copy(src, dst, p_recv.at[group]).start()

            @pl.when(jnp.logical_not(mine))
            def _():
                send(src, dst, p_send, p_recv.at[group], (to_row, owner_col))

    round_y(0, 0)
    across(0, 2, 0)
    inputs_step(0, 1)
    inputs_step(1, 1)
    across(0, 2, 1)
    passing(0)
    passing(1)
    inputs_step(0, 2)
    inputs_step(1, 2)
    across(0, 2, 2)
    own_inputs(2)
    inputs_first(2)
    round_y(0, 1)
    passing(2)
    passing(3)
    inputs_step(0, 3)
    inputs_step(1, 3)
    across(0, 2, 3)
    inputs_step(2, 1)
    across(2, 1, 0)
    across(2, 1, 1)
    own_inputs(3)
    inputs_first(3)
    round_y(0, 2)
    round_y(0, 3)
    passing_last(0)
    passing_last(1)
    inputs_step(0, 4)
    inputs_step(1, 4)
    across(0, 2, 4)
    passing_last(2)
    passing_last(3)
    round_y(1, 0)
    inputs_step(2, 2)
    across(2, 1, 2)
    inputs_step(3, 1)
    across(3, 1, 0)
    across(3, 1, 1)
    round_y(1, 1)
    inputs_step(2, 3)
    across(2, 1, 3)
    inputs_ready(0, 2)
    for parity in range(2):
        errors_ready(1 - x_lo, parity)

    @pl.loop(0, 2)
    def _(j):
        partial_sums(j)

    inputs_step(3, 2)
    across(3, 1, 2)
    round_y(1, 2)
    round_y(1, 3)
    inputs_step(2, 4)
    across(2, 1, 4)
    inputs_step(3, 3)
    across(3, 1, 3)
    inputs_ready(2, 1)
    partial_sums(2)
    errors_ready(x_lo, 1 - near)

    whole_sums(0)
    to_owners(0, 1, 0)

    inputs_step(3, 4)
    across(3, 1, 4)
    inputs_ready(3, 1)
    partial_sums(3)

    whole_sums(1)
    to_owners(1, 1, 0)


    @pl.loop(2, 4)
    def _(j):
        whole_sums(j)
        to_owners(j, 1, j - 1)

    for k, ref in enumerate((*w_old, *b_old)):
        arrived(ref, load.at[k])

    def update(old, out, at, gradient):
        for ref, new in zip(out, adam_update(*(ref[at] for ref in old), gradient)):
            ref[at] = new

    @pl.loop(0, 8)
    def _(t):
        units = pl.ds(pl.multiple_of(128 * t, 128), 128)
        update(w_old, w_out, (slice(None), units), gt[pl.ds(4 * t, 4)].reshape(128, 256).T)

    def update_feedback(first, rows):
        @pl.loop(0, 8)
        def _(g):
            at = (g, pl.ds(first, rows))
            update(b_old, b_out, at, gb_ref[at])

    sent(ibuf.at[0, 0:7], i_send.at[0])
    sent(ibuf.at[0, 0:7], i_send.at[1])
    for j, count in ((0, 2), (2, 1), (3, 1)):
        sent(ibuf.at[pl.ds(j, count), :, 0], sib_send.at[j])
    for j in range(4):
        sent(psend.at[j], rs_send.at[j])
    for h in range(2):
        sent(rbuf, x_send.at[h])
    sent(ebuf.at[0, 0:3], y_send.at[0])

    @pl.when(same)
    def _():
        sent(rbuf, y_send.at[1])
        sent(rbuf.at[0], d_send)

    @pl.when(other)
    def _():
        sent(rbuf.at[0], y_send.at[1])

    @pl.when(at_home)
    def _():
        sent(gt.at[0:31], p_send)

    @pl.when(jnp.logical_not(at_home))
    def _():
        sent(gt, p_send)

    arrived(gb_ref.at[:, pl.ds(0, 16)], p_recv.at[0])
    update_feedback(0, 16)
    for k in (1, 2):
        arrived(gb_ref.at[:, pl.ds(8 + 8 * k, 8)], p_recv.at[k])
        update_feedback(8 + 8 * k, 8)


def store_kernel(*refs):
    copies = [pltpu.make_async_copy(refs[k], refs[8 + k], refs[16].at[k]) for k in range(8)]
    for copy in copies:
        copy.start()
    for copy in copies:
        copy.wait()


def shards(errors, inputs, *states):
    dma = pltpu.SemaphoreType.DMA
    old = [pltpu.VMEM(state.shape, state.dtype) for state in states]
    new = [
        jax.ShapeDtypeStruct(states[k].shape, dtype)
        for k in (0, 3)
        for dtype in (jnp.float32, jnp.bfloat16, jnp.bfloat16, jnp.bfloat16)
    ]
    results = pl.pallas_call(
        update_kernel,
        out_shape=new,
        in_specs=[pl.BlockSpec(memory_space=pltpu.HBM)] * 8,
        out_specs=[pl.BlockSpec(memory_space=pltpu.VMEM)] * 8,
        scratch_shapes=old + [
            pltpu.VMEM((256, 1024), jnp.bfloat16),
            pltpu.VMEM((8, 32, 1024), jnp.float32),
            dma((7,)),
            pltpu.VMEM((4, 8, 2, 256, 256), jnp.bfloat16),
            pltpu.VMEM((2, 4, 4, 256, 256), jnp.bfloat16),
            pltpu.VMEM((2, 4, 256, 256), jnp.bfloat16),
            pltpu.VMEM((32, 32, 256), jnp.float32),
            pltpu.VMEM((4, 256, 256), jnp.float32),
            pltpu.VMEM((4, 256, 256), jnp.float32),
            dma((4, 8, 2)), dma((2,)), dma((4,)), dma((4,)),
            dma((2, 4, 4)), dma((2, 4)), dma, dma((2,)), dma((2,)),
            dma((4,)), dma((4,)), dma((3,)), dma,
        ],
        compiler_params=pltpu.CompilerParams(
            collective_id=0, has_side_effects=True, vmem_limit_bytes=36 << 20
        ),
        cost_estimate=pl.CostEstimate(flops=1 << 36, bytes_accessed=1 << 27, transcendentals=0),
        name="gradients",
    )(*(pltpu.with_memory_space_constraint(array, pltpu.HBM) for array in (errors, inputs, *states)))
    return pl.pallas_call(
        store_kernel,
        out_shape=new,
        in_specs=[pl.BlockSpec(memory_space=pltpu.VMEM)] * 8,
        out_specs=[pl.BlockSpec(memory_space=pltpu.HBM)] * 8,
        scratch_shapes=[dma((8,))],
        compiler_params=pltpu.CompilerParams(vmem_limit_bytes=8 << 20),
        name="store",
    )(*results)


def solution(mesh):
    whole, parts = P("row", "col"), P(None, "row", "col")
    return jax.shard_map(
        shards,
        mesh=mesh,
        in_specs=(P("col", "row"), whole, whole, whole, whole, parts, parts, parts),
        out_specs=(whole,) * 4 + (parts,) * 4,
        check_vma=False,
    )
```
